32 devices in a mesh: row: 4 (over x, core), col: 2 (over y), date: 4 (over z).
Axes of the slice: x: 2, y: 2, z: 4, core: 2. Of those that a mesh axis runs over, the one named last changes fastest.
Arguments:
- slc: bfloat16 [2, 48, 24, 512], P(None, 'date', 'row', 'col'), may hold values from -6 to 6
- pairs: int32 [32, 2], P('date'), may hold values from 0 to 47, as said below
- target: float32 [2, 32, 12, 128], P(None, 'date', 'row', 'col'), may hold values from -4 to 4
- w_lift: bfloat16 [2, 3, 3, 64], replicated, may hold values from -1.5 to 1.5
- b_lift: bfloat16 [2, 64], replicated, may hold values from -2 to 2
- w_mid: bfloat16 [2, 3, 3, 64, 64], replicated, may hold values from -0.1875 to 0.1875
- b_mid: bfloat16 [2, 64], replicated, may hold values from -2 to 2
- w_proj: bfloat16 [2, 3, 3, 64], replicated, may hold values from -0.1875 to 0.1875
Outputs:
- denoised: float32 [2, 32, 12, 128], P(None, 'date', 'row', 'col')
- grad_lift: float32 [2, 3, 3, 64], replicated
- grad_lift_bias: float32 [2, 64], replicated
- grad_mid: float32 [2, 3, 3, 64, 64], replicated
- grad_mid_bias: float32 [2, 64], replicated
- grad_proj: float32 [2, 3, 3, 64], replicated
The draws below stay inside these ranges and needn't reach their ends.
Inputs may be any that keep to these rules, and one draw needn't show every extreme that they name: `pairs`: row p belongs to date index p // 8, which holds dates d * 12 to (d + 1) * 12 - 1; its earlier date lies there, and its later date is later by 1 to 24 dates. Row 0 is (0, 24).
All inputs are finite; a program needn't handle non-finite values.
Results may differ from the reference program's by a relative error of at most 0.00065.
The reference program's roundings to bfloat16 on the way count: a program that leaves them out, or rounds other values in their place, can miss the bound.
Values may be sent and summed in bfloat16 or wider, within the bound.
A program may use at most 64 MiB of HBM per device.

```python
import math
import jax
import jax.numpy as jnp
from jax import lax

CH = 64
PAIRS_DEV = 8
DD = 12
LR = 2
LC = 4
DATES = 48
PAIRS = 32
NR = 24
NC = 512
NMR = 12
NMC = 128
N_DATE = 4


def draw_pairs(key, part):
    row_count = PAIRS_DEV * N_DATE
    holder = jnp.arange(row_count, dtype=jnp.int32) // PAIRS_DEV
    key_early, key_late = jax.random.split(jax.random.fold_in(key, 7))
    slab_start = holder * DD
    slab_stop = jnp.minimum(slab_start + DD, DATES - 1)
    window = slab_stop - slab_start
    earlier = slab_start + jax.random.randint(key_early, (row_count,), 0, 1 << 20, dtype=jnp.int32) % window
    headroom = jnp.minimum(2 * DD, DATES - 1 - earlier)
    later_date = earlier + 1 + jax.random.randint(key_late, (row_count,), 0, 1 << 20, dtype=jnp.int32) % headroom
    earlier = earlier.at[0].set(0)
    later_date = later_date.at[0].set(2 * DD)
    return jnp.stack([earlier, later_date], axis=1).astype(jnp.int32)


def levels(own_key, dims, cuts, smallest, largest):
    loudness, own = 1.0, jax.random.fold_in(own_key, 6)
    for axis_at, parts in cuts:
        draws = jnp.exp(jax.random.uniform(jax.random.fold_in(own, axis_at), (parts,), jnp.float32, smallest / len(cuts), largest / len(cuts)))
        loudness = loudness * jnp.repeat(draws, dims[axis_at] // parts).reshape([-1 if axis == axis_at else 1 for axis in range(len(dims))])
    return loudness


def gaussian(rng, extent, deviation, limit, pieces=(), kind=jnp.bfloat16):
    drawn = deviation * jax.random.normal(rng, extent, jnp.float32)
    if pieces:
        drawn = drawn * levels(rng, extent, pieces, -0.22, 0.18)
    return jnp.clip(drawn, -limit, limit).astype(kind)


def setup_inputs(seed: int = 0) -> dict:
    keys = jax.random.split(jax.random.key(seed), 9)
    return {
        "slc": gaussian(keys[0], (2, DATES, NR, NC), 1.0, 6.0, ((1, 4), (2, 4), (3, 2))),
        "pairs": draw_pairs(jax.random.fold_in(keys[8], 71), 0),
        "target": gaussian(keys[2], (2, PAIRS, NMR, NMC), 0.5, 4.0, ((1, 4), (2, 4), (3, 2)), jnp.float32),
        "w_lift": gaussian(keys[3], (2, 3, 3, CH), 18 ** -0.5, 1.5),
        "b_lift": gaussian(keys[4], (2, CH), 0.3, 2.0),
        "w_mid": gaussian(keys[5], (2, 3, 3, CH, CH), (18 * CH) ** -0.5, 0.1875),
        "b_mid": gaussian(keys[6], (2, CH), 0.3, 2.0),
        "w_proj": gaussian(keys[7], (2, 3, 3, CH), (18 * CH) ** -0.5, 0.1875),
    }


def real_block(weights):
    real_part = weights[0]
    imag_part = weights[1]
    upper = jnp.concatenate([real_part, imag_part], axis=-1)
    lower = jnp.concatenate([-imag_part, real_part], axis=-1)
    return jnp.concatenate([upper, lower], axis=-2)

def fold_grads(gram, inner):
    outer = gram.shape[-1] // 2
    real_part = gram[:, :, :inner, :outer] + gram[:, :, inner:, outer:]
    imag_part = gram[:, :, :inner, outer:] - gram[:, :, inner:, :outer]
    return jnp.stack([real_part, imag_part])

def field_pad(field):
    return jnp.pad(field, ((0, 0), (0, 0), (1, 1), (1, 1)))

def hidden_pad(hidden):
    return jnp.pad(hidden, ((0, 0), (1, 1), (1, 1), (0, 0)))

def tap_sum(padded_in, kernel, form, offset, on_field):
    height = padded_in.shape[2] - 2 if on_field else padded_in.shape[1] - 2
    breadth = padded_in.shape[3] - 2 if on_field else padded_in.shape[2] - 2
    summed = 0.0
    for row_tap in range(3):
        for col_tap in range(3):
            row_at = 2 - row_tap if offset else row_tap
            col_at = 2 - col_tap if offset else col_tap
            if on_field:
                window = padded_in[:, :, row_at:row_at + height, col_at:col_at + breadth]
            else:
                window = padded_in[:, row_at:row_at + height, col_at:col_at + breadth, :]
            summed = summed + jnp.einsum(form, window.astype(jnp.float32), kernel[row_tap, col_tap].astype(jnp.float32))
    return summed

def tap_gram(padded_in, grad_out, form, on_field):
    height = padded_in.shape[2] - 2 if on_field else padded_in.shape[1] - 2
    breadth = padded_in.shape[3] - 2 if on_field else padded_in.shape[2] - 2
    grams = []
    for row_tap in range(3):
        for col_tap in range(3):
            if on_field:
                window = padded_in[:, :, row_tap:row_tap + height, col_tap:col_tap + breadth]
            else:
                window = padded_in[:, row_tap:row_tap + height, col_tap:col_tap + breadth, :]
            grams.append(jnp.einsum(form, window.astype(jnp.float32), grad_out.astype(jnp.float32)))
    stacked = jnp.stack(grams)
    return stacked.reshape((3, 3) + stacked.shape[1:])

def reference(slc, pairs, target, w_lift, b_lift, w_mid, b_mid, w_proj):
    earlier = jnp.take(slc, pairs[:, 0], axis=1).astype(jnp.float32)
    later_date = jnp.take(slc, pairs[:, 1], axis=1).astype(jnp.float32)
    real_part = earlier[0] * later_date[0] + earlier[1] * later_date[1]
    imag_part = earlier[1] * later_date[0] - earlier[0] * later_date[1]
    product = jnp.stack([real_part, imag_part])
    looks = product.reshape(2, PAIRS, NMR, LR, NMC, LC).mean(axis=(3, 5)).astype(jnp.bfloat16)
    lift_block = real_block(w_lift[:, :, :, None, :])
    mid_block = real_block(w_mid)
    proj_block = real_block(w_proj[..., None])
    lift_bias = b_lift.reshape(2 * CH).astype(jnp.float32)
    mid_bias = b_mid.reshape(2 * CH).astype(jnp.float32)
    loss_scale = 1.0 / math.sqrt(2.0 * PAIRS * NMR * NMC)

    def one_pair(inputs):
        image, goal = inputs
        image = image[:, None]
        goal = goal[:, None]
        image_pad = field_pad(image)
        pre1 = tap_sum(image_pad, lift_block, 'zprc,zo->prco', 0, True) + lift_bias
        hidden1 = jnp.maximum(pre1, 0.0).astype(jnp.bfloat16)
        hidden1_pad = hidden_pad(hidden1)
        pre2 = tap_sum(hidden1_pad, mid_block, 'prci,io->prco', 0, False) + mid_bias
        hidden2 = jnp.maximum(pre2, 0.0).astype(jnp.bfloat16)
        hidden2_pad = hidden_pad(hidden2)
        noise = tap_sum(hidden2_pad, proj_block, 'prci,iz->zprc', 0, False)
        cleaned = image.astype(jnp.float32) - noise
        d_noise = ((goal - cleaned) * loss_scale).astype(jnp.bfloat16)
        d_hidden2 = tap_sum(field_pad(d_noise), proj_block, 'zprc,iz->prci', 2, True)
        d_pre2 = jnp.where(hidden2 > 0, d_hidden2, 0.0).astype(jnp.bfloat16)
        d_hidden1 = tap_sum(hidden_pad(d_pre2), mid_block, 'prco,io->prci', 2, False)
        d_pre1 = jnp.where(hidden1 > 0, d_hidden1, 0.0).astype(jnp.bfloat16)
        gram_lift = tap_gram(image_pad, d_pre1, 'zprc,prco->zo', True)
        gram_mid = tap_gram(hidden1_pad, d_pre2, 'prci,prco->io', False)
        gram_proj = tap_gram(hidden2_pad, d_noise, 'prci,zprc->iz', False)
        lift_bias_grad = lax.optimization_barrier(jnp.sum(d_pre1.astype(jnp.float32), axis=(0, 1, 2)))
        mid_bias_grad = lax.optimization_barrier(jnp.sum(d_pre2.astype(jnp.float32), axis=(0, 1, 2)))
        return (cleaned[:, 0], gram_lift, lift_bias_grad, gram_mid, mid_bias_grad, gram_proj)
    results = lax.map(one_pair, (jnp.moveaxis(looks, 1, 0), jnp.moveaxis(target, 1, 0)))
    denoised = jnp.moveaxis(results[0], 0, 1)
    gram_lift = lax.optimization_barrier(jnp.sum(results[1], axis=0))
    lift_bias_grad = lax.optimization_barrier(jnp.sum(results[2], axis=0))
    gram_mid = lax.optimization_barrier(jnp.sum(results[3], axis=0))
    mid_bias_grad = lax.optimization_barrier(jnp.sum(results[4], axis=0))
    gram_proj = lax.optimization_barrier(jnp.sum(results[5], axis=0))
    grad_lift = fold_grads(gram_lift, 1)[:, :, :, 0, :]
    grad_mid = fold_grads(gram_mid, CH)
    grad_proj = fold_grads(gram_proj, CH)[..., 0]
    return (denoised, grad_lift, lift_bias_grad.reshape(2, CH), grad_mid, mid_bias_grad.reshape(2, CH), grad_proj)
```

```python
import functools
import math

import jax
import jax.numpy as jnp
from jax import lax
from jax.experimental import pallas as pl
from jax.experimental.pallas import tpu as pltpu
from jax.sharding import PartitionSpec as P

MESH = pl.DeviceIdType.MESH

LR = 2
LC = 4


def real_block(weights):
    real_part = weights[0]
    imag_part = weights[1]
    upper = jnp.concatenate([real_part, imag_part], axis=-1)
    lower = jnp.concatenate([-imag_part, real_part], axis=-1)
    return jnp.concatenate([upper, lower], axis=-2)


def mm(a, b):
    return jnp.dot(a, b, preferred_element_type=jnp.float32)


def mm_t(a, b):
    return lax.dot_general(a, b, (((1,), (1,)), ((), ())), preferred_element_type=jnp.float32)


def step_kernel(
    dims, scale,
    slc_ref, pick_ref, avg_ref, tgt_ref, w1_ref, wf_ref, bm_ref, wp_ref, wpb_ref, wb_ref,
    den_ref, o_ref,
    pool, look_f, look_s, look_r, tgt_r, fld, tfld, i3a, i3b, h2s, tsum, dn3, dnm3, dp2m, dp1, outs, x_ref,
    plane_in, date_in, slab_sem, look_sem, tgt_sem, den_sem, plane_sem, date_sem, gather_sem,
):
    n_row, n_col, n_date, pp, tr, tc = dims
    r, c, d = lax.axis_index("row"), lax.axis_index("col"), lax.axis_index("date")
    n_plane = n_row * n_col
    me = r * n_col + c
    rows = n_row * tr
    gap = rows + 1
    nb = gap * pp
    n = nb * 128
    base = (128 - tc) // 2
    pairs = pp * n_row
    f32, bf16 = jnp.float32, jnp.bfloat16

    def plane_peer(k):
        peer = lax.rem(me + k, n_plane)
        return peer, (lax.div(peer, n_col), lax.rem(peer, n_col), d)

    def date_peer(k):
        return (r, c, lax.rem(d + k, n_date))

    def remote(src, dst, sems, at, where):
        copy = pltpu.make_async_remote_copy(
            src_ref=src, dst_ref=dst, send_sem=sems.at[0, at], recv_sem=sems.at[1, at],
            device_id=where, device_id_type=MESH,
        )
        copy.start()
        return copy

    barrier = pltpu.get_barrier_semaphore()
    for k in range(1, n_plane):
        pl.semaphore_signal(barrier, inc=1, device_id=plane_peer(k)[1], device_id_type=MESH)
    for k in range(1, n_date):
        pl.semaphore_signal(barrier, inc=1, device_id=date_peer(k), device_id_type=MESH)
    pl.semaphore_wait(barrier, n_plane + n_date - 2)

    sent = []
    slabs = [remote(slc_ref, pool.at[k - 1], slab_sem, k, date_peer(n_date - k)) for k in (1, 2)]

    def exchange(src, dst, sems):
        copies = []
        for way in range(3):
            col = lax.rem(c + (0, 1, n_col - 1)[way], n_col)
            for o in range(n_row):
                k = lax.rem(r + o, n_row)
                at = way * n_row + o
                if way == 0 and o == 0:
                    copy = pltpu.make_async_copy(src.at[k], dst.at[0, r], sems.at[0, at])
                    copy.start()
                    copies.append((copy, True))
                else:
                    copies.append((remote(src.at[k], dst.at[way, r], sems, at, (k, col, d)), False))
        return copies

    tgt_copies = exchange(tgt_ref, tgt_r, tgt_sem)
    for ref in (fld, tfld, dn3, dnm3, tsum):
        ref[...] = jnp.zeros_like(ref)
    edge = jnp.zeros((i3a.shape[0], 128), bf16)
    for ref in (i3a, i3b):
        ref[:, 0:128] = edge
        ref[:, (nb + 1) * 128 : (nb + 2) * 128] = edge
    x_ref[...] = jnp.zeros_like(x_ref)
    lane = lax.broadcasted_iota(jnp.int32, (1, 128), 1)
    spot = c * tc + lane - base
    inside = (spot >= 0) & (spot < n_col * tc)
    own = (lane >= base) & (lane < base + tc)
    for copy in slabs:
        copy.wait_recv()
    sent += slabs

    depth = slc_ref.shape[0]
    picked = (
        mm(pick_ref[:, :depth], slc_ref[...])
        + mm(pick_ref[:, depth : 2 * depth], pool[0])
        + mm(pick_ref[:, 2 * depth :], pool[1])
    )
    parts = slc_ref.shape[1] // (LR * tr)
    halves = tc * LC // parts
    sides = []
    for h in range(halves):
        at = [picked[q * pairs : (q + 1) * pairs] for q in (h, halves + h, 2 * halves + h, 3 * halves + h)]
        a0, a1, b0, b1 = at
        rowsum = []
        for prod in (a0 * b0 + a1 * b1, a1 * b0 - a0 * b1):
            for t in range(tr):
                rowsum.append(
                    sum(prod[:, (t * LR + q) * parts : (t * LR + q + 1) * parts] for q in range(LR))
                )
        sides.append(jnp.concatenate(rowsum, axis=0))
    looked = jnp.dot(
        jnp.concatenate(sides, axis=1), avg_ref[...],
        precision=lax.Precision.HIGHEST, preferred_element_type=f32,
    )
    look_f[...] = jnp.zeros_like(look_f)
    for k in range(n_row):
        for q in range(2 * tr):
            look_f[k, q * pp : (q + 1) * pp, :] = looked[q * pairs + k * pp : q * pairs + (k + 1) * pp]
    look_s[...] = look_f[...].astype(bf16)
    look_copies = exchange(look_s, look_r, look_sem)

    def settle(copies):
        for copy, near in copies:
            if near:
                copy.wait()
            else:
                copy.wait_recv()
                sent.append(copy)

    def assemble(ref, s):
        mid = pltpu.roll(ref[0, s].astype(f32), base, 1)
        low = pltpu.roll(ref[1, s].astype(f32), (base - tc) % 128, 1)
        high = pltpu.roll(ref[2, s].astype(f32), base + tc, 1)
        joined = jnp.where(own, mid, jnp.where(lane < base, low, high))
        near = (lane >= base - 5) & (lane < base + tc + 5)
        return jnp.where(inside & near, joined, 0.0)

    settle(tgt_copies)
    for s in range(n_row):
        block = assemble(tgt_r, s)
        for z in range(2):
            for t in range(tr):
                for p in range(pp):
                    i = (z * tr + t) * pp + p
                    b = p * gap + s * tr + t
                    tfld[z : z + 1, b * 128 : (b + 1) * 128] = block[i : i + 1]
    settle(look_copies)
    for s in range(n_row):
        block = assemble(look_r, s)
        for u, turned in enumerate((pltpu.roll(block, 1, 1), block, pltpu.roll(block, 127, 1))):
            for z in range(2):
                for t in range(tr):
                    for p in range(pp):
                        i = (z * tr + t) * pp + p
                        b = p * gap + s * tr + t + 1
                        fld[2 * u + z : 2 * u + z + 1, b * 128 : (b + 1) * 128] = turned[i : i + 1]
    fld[6:7, :] = jnp.ones((1, (nb + 2) * 128), f32)

    def taps(ref, at, width):
        three = [ref[:, pl.ds(pl.multiple_of(at + t * 128, 128), width)] for t in range(3)]
        return jnp.concatenate(three + [jnp.zeros((8, width), f32)], axis=0).astype(bf16)

    def turned_store(ref, value, at):
        for u, turn in enumerate((1, 0, 127)):
            for q in range(2):
                piece = value[:, q * 128 : (q + 1) * 128]
                if turn:
                    piece = pltpu.roll(piece, turn, 1)
                ref[u * 128 : (u + 1) * 128, pl.ds(pl.multiple_of(at + (q + 1) * 128, 128), 128)] = (
                    piece.astype(bf16)
                )

    def good(b):
        one = [inside & (lax.rem(b + q, gap) != gap - 1) for q in range(2)]
        return jnp.concatenate(one, axis=1)

    own2 = jnp.concatenate([own, own], axis=1)

    def rounded(value):
        return value.astype(bf16).astype(f32)

    def lift(i, carry):
        at = pl.multiple_of(i * 256, 256)
        pre1 = mm(w1_ref[...], taps(fld, at, 256))
        turned_store(i3a, rounded(jnp.where(good(2 * i), jnp.maximum(pre1, 0.0), 0.0)), at)
        return carry

    lax.fori_loop(0, nb // 2, lift, 0)

    def conv(w_ref, ref, at):
        total = 0.0
        for t in range(3):
            total = total + mm(w_ref[t], ref[:, pl.ds(pl.multiple_of(at + t * 128, 128), 256)])
        return total

    def mid(i, carry):
        at = pl.multiple_of(i * 256, 256)
        pre2 = conv(wf_ref, i3a, at) + bm_ref[...]
        h2 = jnp.where(good(2 * i), jnp.maximum(pre2, 0.0), 0.0).astype(bf16)
        h2s[:, pl.ds(at, 256)] = h2
        tsum[:, pl.ds(pl.multiple_of(at + 128, 128), 256)] = mm(wp_ref[...], h2)
        return carry

    lax.fori_loop(0, nb // 2, mid, 0)

    six = sum(tsum[8 * t : 8 * t + 8, t * 128 : t * 128 + n] for t in range(3))
    noise = pltpu.roll(six, 1, 1)[0:2] + six[2:4] + pltpu.roll(six, n - 1, 1)[4:6]
    den = fld[2:4, 128 : 128 + n] - noise
    shifted = pltpu.roll(den, n - base, 1)
    outs[...] = jnp.zeros_like(outs)
    for s in range(n_row):
        for z in range(2):
            for t in range(tr):
                for p in range(pp):
                    i = (z * tr + t) * pp + p
                    b = p * gap + s * tr + t
                    outs[s, i : i + 1, :] = shifted[z : z + 1, b * 128 : (b + 1) * 128]
    den_copies = []
    for o in range(n_row):
        k = lax.rem(r + o, n_row)
        if o == 0:
            copy = pltpu.make_async_copy(outs.at[k], den_ref.at[r], den_sem.at[0, o])
            copy.start()
            den_copies.append((copy, True))
        else:
            den_copies.append((remote(outs.at[k], den_ref.at[r], den_sem, o, (k, c, d)), False))
    dn = rounded((tfld[0:2, :] - den) * scale)
    rowok = [jnp.full((1, 128), b % gap != gap - 1) for b in range(nb)]
    mask = jnp.concatenate([inside & ok for ok in rowok], axis=1)
    own_all = jnp.concatenate([own & ok for ok in rowok], axis=1)
    for ref, keep in ((dn3, mask), (dnm3, own_all)):
        kept = jnp.where(keep, dn, 0.0)
        ref[0:2, 128 : 128 + n] = pltpu.roll(kept, 1, 1)
        ref[2:4, 128 : 128 + n] = kept
        ref[4:6, 128 : 128 + n] = pltpu.roll(kept, n - 1, 1)

    def back2(i, carry):
        at = pl.multiple_of(i * 256, 256)
        grad = mm(wpb_ref[...], taps(dn3, at, 256))
        grad = rounded(jnp.where(h2s[:, pl.ds(at, 256)].astype(f32) > 0, grad, 0.0))
        turned_store(i3b, grad, at)
        dp2m[:, pl.ds(at, 256)] = jnp.where(own2, grad, 0.0).astype(bf16)
        return carry

    lax.fori_loop(0, nb // 2, back2, 0)

    def back1(i, carry):
        at = pl.multiple_of(i * 256, 256)
        h1 = i3a[128:256, pl.ds(pl.multiple_of(at + 128, 128), 256)].astype(f32)
        grad = jnp.where((h1 > 0) & own2, conv(wb_ref, i3b, at), 0.0)
        dp1[:, pl.ds(at, 256)] = grad.astype(bf16)
        return carry

    lax.fori_loop(0, nb // 2, back1, 0)

    sign = jnp.where(lane < 64, 1.0, -1.0)
    for t in range(3):
        gram = mm_t(i3a[:, t * 128 : t * 128 + n], dp2m[...])
        for u in range(3):
            upper = gram[u * 128 : u * 128 + 64]
            lower = gram[u * 128 + 64 : u * 128 + 128]
            x_ref[(3 * t + u) * 64 : (3 * t + u) * 64 + 64, :] = upper + sign * pltpu.roll(lower, 64, 1)
    x_ref[576:600, :] = mm_t(taps(fld, 0, n), dp1[...])[0:24]
    x_ref[600:624, :] = mm_t(taps(dnm3, 0, n), h2s[...])[0:24]
    x_ref[624:632, :] = mm_t(jnp.ones((16, n), bf16), dp2m[...])[0:8]

    piece = plane_in.shape[1]

    def slot(ref, k):
        return ref.at[pl.ds(pl.multiple_of(k * piece, 8), piece)]

    scatter = []
    for k in range(1, n_plane):
        peer, where = plane_peer(k)
        scatter.append(remote(slot(x_ref, peer), plane_in.at[k], plane_sem, k, where))
    part = slot(x_ref, me)[...]
    for k, copy in zip(range(1, n_plane), scatter):
        copy.wait_recv()
        part = part + plane_in[k]
    date_in[d] = part
    spread = [remote(date_in.at[d], date_in.at[d], date_sem, k, date_peer(k)) for k in range(1, n_date)]
    for copy in spread:
        copy.wait_recv()
    slot(o_ref, me)[...] = functools.reduce(lambda a, b: a + b, [date_in[k] for k in range(n_date)])
    gather = [
        remote(slot(o_ref, me), slot(o_ref, me), gather_sem, k, plane_peer(k)[1])
        for k in range(1, n_plane)
    ]
    for copy in gather:
        copy.wait_recv()
    settle(den_copies)
    for copy in sent + scatter + spread + gather:
        copy.wait_send()


def local(slc, pairs, target, w_lift, b_lift, w_mid, b_mid, w_proj):
    n_row, n_col, n_date = (lax.axis_size(axis) for axis in ("row", "col", "date"))
    dates, srows, scols = slc.shape[1:]
    count, tr, tc = target.shape[1:]
    ch = w_mid.shape[-1]
    pp = count // n_row
    halves = scols // 128
    bf16, f32 = jnp.bfloat16, jnp.float32
    rows = 2 * tr * pp
    pad_rows = -(-rows // 16) * 16
    packed = slc.reshape(2, dates, srows, halves, 128).transpose(1, 0, 3, 2, 4)
    packed = packed.reshape(dates * 2 * halves, srows * 128)
    index = (pairs - lax.axis_index("date") * dates).T
    kinds = 2 * halves
    want = (index[:, None, :] * kinds + jnp.arange(kinds, dtype=jnp.int32)[None, :, None]).reshape(-1)
    pick = (want[:, None] == jnp.arange(3 * dates * kinds, dtype=jnp.int32)[None, :]).astype(bf16)
    spots = jnp.arange(scols, dtype=jnp.int32)[:, None] // LC
    avg = jnp.where(spots == jnp.arange(128, dtype=jnp.int32)[None, :], 1.0 / (LR * LC), 0.0).astype(f32)
    tgt = target.reshape(2, n_row, pp, tr, tc).transpose(1, 0, 3, 2, 4).reshape(n_row, rows, tc)
    tgt = jnp.pad(tgt, ((0, 0), (0, pad_rows - rows), (0, 128 - tc)))
    lift = real_block(w_lift[:, :, :, None, :])
    lift = jnp.pad(lift.reshape(3, 6, 2 * ch), ((0, 0), (0, 2), (0, 0)))
    lift = lift.at[1, 6].set(b_lift.reshape(2 * ch))
    w1 = jnp.pad(lift.reshape(24, 2 * ch), ((0, 8), (0, 0))).T
    mid = real_block(w_mid)
    wf = mid.reshape(3, 6 * ch, 2 * ch).transpose(0, 2, 1)
    wb = mid[::-1, ::-1].transpose(0, 2, 1, 3).reshape(3, 2 * ch, 6 * ch)
    proj = real_block(w_proj[..., None])

    def tap_rows(kernel):
        kernel = kernel.transpose(0, 1, 3, 2).reshape(3, 6, 2 * ch)
        kernel = jnp.pad(kernel, ((0, 0), (0, 2), (0, 0))).reshape(24, 2 * ch)
        return jnp.pad(kernel, ((0, 8), (0, 0)))

    wp = tap_rows(proj)
    wpb = tap_rows(proj[::-1, ::-1]).T
    bm = b_mid.reshape(2 * ch, 1).astype(f32)
    scale = 1.0 / math.sqrt(2.0 * count * n_date * tr * n_row * tc * n_col)
    nb = (n_row * tr + 1) * pp
    n, wide = nb * 128, (nb + 2) * 128
    n_plane = n_row * n_col
    piece = -(-632 // (8 * n_plane)) * 8
    dma = pltpu.SemaphoreType.DMA
    vmem = pltpu.VMEM
    den, sums = pl.pallas_call(
        functools.partial(step_kernel, (n_row, n_col, n_date, pp, tr, tc), scale),
        out_shape=(
            jax.ShapeDtypeStruct((n_row, pad_rows, 128), f32),
            jax.ShapeDtypeStruct((n_plane * piece, 128), f32),
        ),
        in_specs=[pl.BlockSpec(memory_space=vmem)] * 10,
        out_specs=(pl.BlockSpec(memory_space=vmem),) * 2,
        scratch_shapes=[
            vmem((2,) + packed.shape, bf16),
            vmem((n_row, pad_rows, 128), f32),
            vmem((n_row, pad_rows, 128), bf16),
            vmem((3, n_row, pad_rows, 128), bf16),
            vmem((3, n_row, pad_rows, 128), f32),
            vmem((8, wide), f32),
            vmem((8, n), f32),
            vmem((6 * ch, wide), bf16),
            vmem((6 * ch, wide), bf16),
            vmem((2 * ch, n), bf16),
            vmem((32, wide), f32),
            vmem((8, wide), f32),
            vmem((8, wide), f32),
            vmem((2 * ch, n), bf16),
            vmem((2 * ch, n), bf16),
            vmem((n_row, pad_rows, 128), f32),
            vmem((n_plane * piece, 128), f32),
            vmem((n_plane, piece, 128), f32),
            vmem((n_date, piece, 128), f32),
            dma((2, 3)),
            dma((2, 3 * n_row)),
            dma((2, 3 * n_row)),
            dma((2, n_row)),
            dma((2, n_plane)),
            dma((2, n_date)),
            dma((2, n_plane)),
        ],
        compiler_params=pltpu.CompilerParams(
            collective_id=0, has_side_effects=True, vmem_limit_bytes=48 * 1024 * 1024
        ),
    )(packed, pick, avg, tgt, w1, wf, bm, wp, wpb, wb)
    denoised = den[:, :rows, :tc].reshape(n_row, 2, tr, pp, tc).transpose(1, 0, 3, 2, 4)
    denoised = denoised.reshape(2, count, tr, tc)
    grad_mid = sums[: 9 * ch].reshape(3, 3, ch, 2, ch).transpose(3, 0, 1, 2, 4)
    g_lift = sums[576:600].reshape(3, 8, 2 * ch)
    lift_bias = g_lift[1, 6]
    g_lift = g_lift[:, :6].reshape(3, 3, 2, 2, ch)
    grad_lift = jnp.stack(
        [g_lift[:, :, 0, 0] + g_lift[:, :, 1, 1], g_lift[:, :, 0, 1] - g_lift[:, :, 1, 0]]
    )
    g_proj = sums[600:624].reshape(3, 8, 2 * ch)[:, :6].reshape(3, 3, 2, 2, ch)[::-1, ::-1]
    grad_proj = jnp.stack(
        [g_proj[:, :, 0, 0] + g_proj[:, :, 1, 1], g_proj[:, :, 1, 0] - g_proj[:, :, 0, 1]]
    )
    return (
        denoised,
        grad_lift,
        lift_bias.reshape(2, ch),
        grad_mid,
        sums[624].reshape(2, ch),
        grad_proj,
    )


def solution(mesh):
    in_specs = (
        P(None, "date", "row", "col"),
        P("date", None),
        P(None, "date", "row", "col"),
        P(),
        P(),
        P(),
        P(),
        P(),
    )
    out_specs = (P(None, "date", "row", "col"), P(), P(), P(), P(), P())
    return jax.shard_map(local, mesh=mesh, in_specs=in_specs, out_specs=out_specs, check_vma=False)
```

```python
import functools
import math

import jax
import jax.numpy as jnp
from jax import lax
from jax.experimental import pallas as pl
from jax.experimental.pallas import tpu as pltpu
from jax.sharding import PartitionSpec as P

MESH = pl.DeviceIdType.MESH

LR = 2
LC = 4


def real_block(weights):
    real_part = weights[0]
    imag_part = weights[1]
    upper = jnp.concatenate([real_part, imag_part], axis=-1)
    lower = jnp.concatenate([-imag_part, real_part], axis=-1)
    return jnp.concatenate([upper, lower], axis=-2)


def mm(a, b):
    return jnp.dot(a, b, preferred_element_type=jnp.float32)


def mm_t(a, b):
    return lax.dot_general(a, b, (((1,), (1,)), ((), ())), preferred_element_type=jnp.float32)


def step_kernel(
    dims, scale,
    slc_ref, pick_ref, avg_ref, tgt_ref, w1_ref, wf_ref, bm_ref, wp_ref, wpb_ref, wb_ref,
    den_ref, o_ref, small_ref,
    pool, look_f, look_s, look_r, tgt_r, fld, tfld, i3a, i3b, h2s, tsum, dn3, dnm3, dp2m, dp1, outs, x_ref,
    plane_in, date_in, small_in, small_date, small_sem, small_date_sem, slab_sem, look_sem, tgt_sem, den_sem, plane_sem, date_sem, gather_sem,
):
    n_row, n_col, n_date, pp, tr, tc = dims
    r, c, d = lax.axis_index("row"), lax.axis_index("col"), lax.axis_index("date")
    n_plane = n_row * n_col
    me = r * n_col + c
    rows = n_row * tr
    gap = rows + 1
    nb = gap * pp
    n = nb * 128
    base = (128 - tc) // 2
    pairs = pp * n_row
    f32, bf16 = jnp.float32, jnp.bfloat16

    def plane_peer(k):
        peer = lax.rem(me + k, n_plane)
        return peer, (lax.div(peer, n_col), lax.rem(peer, n_col), d)

    def date_peer(k):
        return (r, c, lax.rem(d + k, n_date))

    def remote(src, dst, sems, at, where):
        copy = pltpu.make_async_remote_copy(
            src_ref=src, dst_ref=dst, send_sem=sems.at[0, at], recv_sem=sems.at[1, at],
            device_id=where, device_id_type=MESH,
        )
        copy.start()
        return copy

    barrier = pltpu.get_barrier_semaphore()
    for k in range(1, n_plane):
        pl.semaphore_signal(barrier, inc=1, device_id=plane_peer(k)[1], device_id_type=MESH)
    for k in range(1, n_date):
        pl.semaphore_signal(barrier, inc=1, device_id=date_peer(k), device_id_type=MESH)
    pl.semaphore_wait(barrier, n_plane + n_date - 2)

    sent = []
    slabs = [remote(slc_ref, pool.at[k - 1], slab_sem, k, date_peer(n_date - k)) for k in (1, 2)]

    def exchange(src, dst, sems):
        copies = []
        for way in range(3):
            col = lax.rem(c + (0, 1, n_col - 1)[way], n_col)
            for o in range(n_row):
                k = lax.rem(r + o, n_row)
                at = way * n_row + o
                if way == 0 and o == 0:
                    copy = pltpu.make_async_copy(src.at[k], dst.at[0, r], sems.at[0, at])
                    copy.start()
                    copies.append((copy, True))
                else:
                    copies.append((remote(src.at[k], dst.at[way, r], sems, at, (k, col, d)), False))
        return copies

    tgt_copies = exchange(tgt_ref, tgt_r, tgt_sem)
    for ref in (fld, tfld, dn3, dnm3, tsum):
        ref[...] = jnp.zeros_like(ref)
    edge = jnp.zeros((i3a.shape[0], 128), bf16)
    for ref in (i3a, i3b):
        ref[:, 0:128] = edge
        ref[:, (nb + 1) * 128 : (nb + 2) * 128] = edge
    x_ref[...] = jnp.zeros_like(x_ref)
    lane = lax.broadcasted_iota(jnp.int32, (1, 128), 1)
    spot = c * tc + lane - base
    inside = (spot >= 0) & (spot < n_col * tc)
    own = (lane >= base) & (lane < base + tc)
    for copy in slabs:
        copy.wait_recv()
    sent += slabs

    depth = slc_ref.shape[0]
    picked = (
        mm(pick_ref[:, :depth], slc_ref[...])
        + mm(pick_ref[:, depth : 2 * depth], pool[0])
        + mm(pick_ref[:, 2 * depth :], pool[1])
    )
    parts = slc_ref.shape[1] // (LR * tr)
    halves = tc * LC // parts
    sides = []
    for h in range(halves):
        at = [picked[q * pairs : (q + 1) * pairs] for q in (h, halves + h, 2 * halves + h, 3 * halves + h)]
        a0, a1, b0, b1 = at
        rowsum = []
        for prod in (a0 * b0 + a1 * b1, a1 * b0 - a0 * b1):
            for t in range(tr):
                rowsum.append(
                    sum(prod[:, (t * LR + q) * parts : (t * LR + q + 1) * parts] for q in range(LR))
                )
        sides.append(jnp.concatenate(rowsum, axis=0))
    looked = jnp.dot(
        jnp.concatenate(sides, axis=1), avg_ref[...],
        precision=lax.Precision.HIGHEST, preferred_element_type=f32,
    )
    look_f[...] = jnp.zeros_like(look_f)
    for k in range(n_row):
        for q in range(2 * tr):
            look_f[k, q * pp : (q + 1) * pp, :] = looked[q * pairs + k * pp : q * pairs + (k + 1) * pp]
    look_s[...] = look_f[...].astype(bf16)
    look_copies = exchange(look_s, look_r, look_sem)

    def settle(copies):
        for copy, near in copies:
            if near:
                copy.wait()
            else:
                copy.wait_recv()
                sent.append(copy)

    def assemble(ref, s):
        mid = pltpu.roll(ref[0, s].astype(f32), base, 1)
        low = pltpu.roll(ref[1, s].astype(f32), (base - tc) % 128, 1)
        high = pltpu.roll(ref[2, s].astype(f32), base + tc, 1)
        joined = jnp.where(own, mid, jnp.where(lane < base, low, high))
        near = (lane >= base - 5) & (lane < base + tc + 5)
        return jnp.where(inside & near, joined, 0.0)

    settle(tgt_copies)
    for s in range(n_row):
        block = assemble(tgt_r, s)
        for z in range(2):
            for t in range(tr):
                for p in range(pp):
                    i = (z * tr + t) * pp + p
                    b = p * gap + s * tr + t
                    tfld[z : z + 1, b * 128 : (b + 1) * 128] = block[i : i + 1]
    settle(look_copies)
    for s in range(n_row):
        block = assemble(look_r, s)
        for u, turned in enumerate((pltpu.roll(block, 1, 1), block, pltpu.roll(block, 127, 1))):
            for z in range(2):
                for t in range(tr):
                    for p in range(pp):
                        i = (z * tr + t) * pp + p
                        b = p * gap + s * tr + t + 1
                        fld[2 * u + z : 2 * u + z + 1, b * 128 : (b + 1) * 128] = turned[i : i + 1]
    fld[6:7, :] = jnp.ones((1, (nb + 2) * 128), f32)

    def taps(ref, at, width):
        three = [ref[:, pl.ds(pl.multiple_of(at + t * 128, 128), width)] for t in range(3)]
        return jnp.concatenate(three + [jnp.zeros((8, width), f32)], axis=0).astype(bf16)

    def turned_store(ref, value, at):
        for u, turn in enumerate((1, 0, 127)):
            for q in range(2):
                piece = value[:, q * 128 : (q + 1) * 128]
                if turn:
                    piece = pltpu.roll(piece, turn, 1)
                ref[u * 128 : (u + 1) * 128, pl.ds(pl.multiple_of(at + (q + 1) * 128, 128), 128)] = (
                    piece.astype(bf16)
                )

    def good(b):
        one = [inside & (lax.rem(b + q, gap) != gap - 1) for q in range(2)]
        return jnp.concatenate(one, axis=1)

    own2 = jnp.concatenate([own, own], axis=1)

    def rounded(value):
        return value.astype(bf16).astype(f32)

    def lift(i, carry):
        at = pl.multiple_of(i * 256, 256)
        pre1 = mm(w1_ref[...], taps(fld, at, 256))
        turned_store(i3a, rounded(jnp.where(good(2 * i), jnp.maximum(pre1, 0.0), 0.0)), at)
        return carry

    lax.fori_loop(0, nb // 2, lift, 0, unroll=True)

    def conv(w_ref, ref, at):
        total = 0.0
        for t in range(3):
            total = total + mm(w_ref[t], ref[:, pl.ds(pl.multiple_of(at + t * 128, 128), 256)])
        return total

    def mid(i, carry):
        at = pl.multiple_of(i * 256, 256)
        pre2 = conv(wf_ref, i3a, at) + bm_ref[...]
        h2 = jnp.where(good(2 * i), jnp.maximum(pre2, 0.0), 0.0).astype(bf16)
        h2s[:, pl.ds(at, 256)] = h2
        tsum[:, pl.ds(pl.multiple_of(at + 128, 128), 256)] = mm(wp_ref[...], h2)
        return carry

    lax.fori_loop(0, nb // 2, mid, 0, unroll=True)

    six = sum(tsum[8 * t : 8 * t + 8, t * 128 : t * 128 + n] for t in range(3))
    noise = pltpu.roll(six, 1, 1)[0:2] + six[2:4] + pltpu.roll(six, n - 1, 1)[4:6]
    den = fld[2:4, 128 : 128 + n] - noise
    shifted = pltpu.roll(den, n - base, 1)
    outs[...] = jnp.zeros_like(outs)
    for s in range(n_row):
        for z in range(2):
            for t in range(tr):
                for p in range(pp):
                    i = (z * tr + t) * pp + p
                    b = p * gap + s * tr + t
                    outs[s, i : i + 1, :] = shifted[z : z + 1, b * 128 : (b + 1) * 128]
    den_copies = []
    for o in range(n_row):
        k = lax.rem(r + o, n_row)
        if o == 0:
            copy = pltpu.make_async_copy(outs.at[k], den_ref.at[r], den_sem.at[0, o])
            copy.start()
            den_copies.append((copy, True))
        else:
            den_copies.append((remote(outs.at[k], den_ref.at[r], den_sem, o, (k, c, d)), False))
    dn = rounded((tfld[0:2, :] - den) * scale)
    rowok = [jnp.full((1, 128), b % gap != gap - 1) for b in range(nb)]
    mask = jnp.concatenate([inside & ok for ok in rowok], axis=1)
    own_all = jnp.concatenate([own & ok for ok in rowok], axis=1)
    for ref, keep in ((dn3, mask), (dnm3, own_all)):
        kept = jnp.where(keep, dn, 0.0)
        ref[0:2, 128 : 128 + n] = pltpu.roll(kept, 1, 1)
        ref[2:4, 128 : 128 + n] = kept
        ref[4:6, 128 : 128 + n] = pltpu.roll(kept, n - 1, 1)

    def back2(i, carry):
        at = pl.multiple_of(i * 256, 256)
        grad = mm(wpb_ref[...], taps(dn3, at, 256))
        grad = rounded(jnp.where(h2s[:, pl.ds(at, 256)].astype(f32) > 0, grad, 0.0))
        turned_store(i3b, grad, at)
        dp2m[:, pl.ds(at, 256)] = jnp.where(own2, grad, 0.0).astype(bf16)
        return carry

    lax.fori_loop(0, nb // 2, back2, 0, unroll=True)

    sign = jnp.where(lane < 64, 1.0, -1.0)
    for t in range(3):
        gram = mm_t(i3a[:, t * 128 : t * 128 + n], dp2m[...])
        for u in range(3):
            upper = gram[u * 128 : u * 128 + 64]
            lower = gram[u * 128 + 64 : u * 128 + 128]
            x_ref[(3 * t + u) * 64 : (3 * t + u) * 64 + 64, :] = upper + sign * pltpu.roll(lower, 64, 1)
    x_ref[576:600, :] = mm_t(taps(dnm3, 0, n), h2s[...])[0:24]
    x_ref[600:608, :] = mm_t(jnp.ones((16, n), bf16), dp2m[...])[0:8]

    piece = plane_in.shape[1]

    def slot(ref, k):
        return ref.at[pl.ds(pl.multiple_of(k * piece, 8), piece)]

    scatter = []
    for k in range(1, n_plane):
        peer, where = plane_peer(k)
        scatter.append(remote(slot(x_ref, peer), plane_in.at[k], plane_sem, k, where))

    def back1(i, carry):
        at = pl.multiple_of(i * 256, 256)
        h1 = i3a[128:256, pl.ds(pl.multiple_of(at + 128, 128), 256)].astype(f32)
        grad = jnp.where((h1 > 0) & own2, conv(wb_ref, i3b, at), 0.0)
        dp1[:, pl.ds(at, 256)] = grad.astype(bf16)
        return carry

    lax.fori_loop(0, nb // 2, back1, 0, unroll=True)

    small_in[me] = mm_t(taps(fld, 0, n), dp1[...])[0:24]
    small = [
        remote(small_in.at[me], small_in.at[me], small_sem, k, plane_peer(k)[1]) for k in range(1, n_plane)
    ]
    part = slot(x_ref, me)[...]
    for k, copy in zip(range(1, n_plane), scatter):
        copy.wait_recv()
        part = part + plane_in[k]
    date_in[d] = part
    spread = [remote(date_in.at[d], date_in.at[d], date_sem, k, date_peer(k)) for k in range(1, n_date)]

    def total(ref, count):
        return functools.reduce(lambda a, b: a + b, [ref[k] for k in range(count)])

    for copy in small:
        copy.wait_recv()
    small_date[d] = total(small_in, n_plane)
    small_spread = [
        remote(small_date.at[d], small_date.at[d], small_date_sem, k, date_peer(k)) for k in range(1, n_date)
    ]
    for copy in spread:
        copy.wait_recv()
    slot(o_ref, me)[...] = total(date_in, n_date)
    gather = [
        remote(slot(o_ref, me), slot(o_ref, me), gather_sem, k, plane_peer(k)[1])
        for k in range(1, n_plane)
    ]
    for copy in small_spread:
        copy.wait_recv()
    small_ref[...] = total(small_date, n_date)
    settle(den_copies)
    for copy in gather:
        copy.wait_recv()
    for copy in sent + scatter + small + spread + small_spread + gather:
        copy.wait_send()


def local(slc, pairs, target, w_lift, b_lift, w_mid, b_mid, w_proj):
    n_row, n_col, n_date = (lax.axis_size(axis) for axis in ("row", "col", "date"))
    dates, srows, scols = slc.shape[1:]
    count, tr, tc = target.shape[1:]
    ch = w_mid.shape[-1]
    pp = count // n_row
    halves = scols // 128
    bf16, f32 = jnp.bfloat16, jnp.float32
    rows = 2 * tr * pp
    pad_rows = -(-rows // 16) * 16
    packed = slc.reshape(2, dates, srows, halves, 128).transpose(1, 0, 3, 2, 4)
    packed = packed.reshape(dates * 2 * halves, srows * 128)
    index = (pairs - lax.axis_index("date") * dates).T
    kinds = 2 * halves
    want = (index[:, None, :] * kinds + jnp.arange(kinds, dtype=jnp.int32)[None, :, None]).reshape(-1)
    pick = (want[:, None] == jnp.arange(3 * dates * kinds, dtype=jnp.int32)[None, :]).astype(bf16)
    spots = jnp.arange(scols, dtype=jnp.int32)[:, None] // LC
    avg = jnp.where(spots == jnp.arange(128, dtype=jnp.int32)[None, :], 1.0 / (LR * LC), 0.0).astype(f32)
    tgt = target.reshape(2, n_row, pp, tr, tc).transpose(1, 0, 3, 2, 4).reshape(n_row, rows, tc)
    tgt = jnp.pad(tgt, ((0, 0), (0, pad_rows - rows), (0, 128 - tc)))
    lift = real_block(w_lift[:, :, :, None, :])
    lift = jnp.pad(lift.reshape(3, 6, 2 * ch), ((0, 0), (0, 2), (0, 0)))
    lift = lift.at[1, 6].set(b_lift.reshape(2 * ch))
    w1 = jnp.pad(lift.reshape(24, 2 * ch), ((0, 8), (0, 0))).T
    mid = real_block(w_mid)
    wf = mid.reshape(3, 6 * ch, 2 * ch).transpose(0, 2, 1)
    wb = mid[::-1, ::-1].transpose(0, 2, 1, 3).reshape(3, 2 * ch, 6 * ch)
    proj = real_block(w_proj[..., None])

    def tap_rows(kernel):
        kernel = kernel.transpose(0, 1, 3, 2).reshape(3, 6, 2 * ch)
        kernel = jnp.pad(kernel, ((0, 0), (0, 2), (0, 0))).reshape(24, 2 * ch)
        return jnp.pad(kernel, ((0, 8), (0, 0)))

    wp = tap_rows(proj)
    wpb = tap_rows(proj[::-1, ::-1]).T
    bm = b_mid.reshape(2 * ch, 1).astype(f32)
    scale = 1.0 / math.sqrt(2.0 * count * n_date * tr * n_row * tc * n_col)
    nb = (n_row * tr + 1) * pp
    n, wide = nb * 128, (nb + 2) * 128
    n_plane = n_row * n_col
    piece = -(-608 // (8 * n_plane)) * 8
    dma = pltpu.SemaphoreType.DMA
    vmem = pltpu.VMEM
    den, sums, small = pl.pallas_call(
        functools.partial(step_kernel, (n_row, n_col, n_date, pp, tr, tc), scale),
        out_shape=(
            jax.ShapeDtypeStruct((n_row, pad_rows, 128), f32),
            jax.ShapeDtypeStruct((n_plane * piece, 128), f32),
            jax.ShapeDtypeStruct((24, 128), f32),
        ),
        in_specs=[pl.BlockSpec(memory_space=vmem)] * 10,
        out_specs=(pl.BlockSpec(memory_space=vmem),) * 3,
        scratch_shapes=[
            vmem((2,) + packed.shape, bf16),
            vmem((n_row, pad_rows, 128), f32),
            vmem((n_row, pad_rows, 128), bf16),
            vmem((3, n_row, pad_rows, 128), bf16),
            vmem((3, n_row, pad_rows, 128), f32),
            vmem((8, wide), f32),
            vmem((8, n), f32),
            vmem((6 * ch, wide), bf16),
            vmem((6 * ch, wide), bf16),
            vmem((2 * ch, n), bf16),
            vmem((32, wide), f32),
            vmem((8, wide), f32),
            vmem((8, wide), f32),
            vmem((2 * ch, n), bf16),
            vmem((2 * ch, n), bf16),
            vmem((n_row, pad_rows, 128), f32),
            vmem((n_plane * piece, 128), f32),
            vmem((n_plane, piece, 128), f32),
            vmem((n_date, piece, 128), f32),
            vmem((n_plane, 24, 128), f32),
            vmem((n_date, 24, 128), f32),
            dma((2, n_plane)),
            dma((2, n_date)),
            dma((2, 3)),
            dma((2, 3 * n_row)),
            dma((2, 3 * n_row)),
            dma((2, n_row)),
            dma((2, n_plane)),
            dma((2, n_date)),
            dma((2, n_plane)),
        ],
        compiler_params=pltpu.CompilerParams(
            collective_id=0, has_side_effects=True, vmem_limit_bytes=48 * 1024 * 1024
        ),
    )(packed, pick, avg, tgt, w1, wf, bm, wp, wpb, wb)
    denoised = den[:, :rows, :tc].reshape(n_row, 2, tr, pp, tc).transpose(1, 0, 3, 2, 4)
    denoised = denoised.reshape(2, count, tr, tc)
    grad_mid = sums[: 9 * ch].reshape(3, 3, ch, 2, ch).transpose(3, 0, 1, 2, 4)
    g_lift = small.reshape(3, 8, 2 * ch)
    lift_bias = g_lift[1, 6]
    g_lift = g_lift[:, :6].reshape(3, 3, 2, 2, ch)
    grad_lift = jnp.stack(
        [g_lift[:, :, 0, 0] + g_lift[:, :, 1, 1], g_lift[:, :, 0, 1] - g_lift[:, :, 1, 0]]
    )
    g_proj = sums[576:600].reshape(3, 8, 2 * ch)[:, :6].reshape(3, 3, 2, 2, ch)[::-1, ::-1]
    grad_proj = jnp.stack(
        [g_proj[:, :, 0, 0] + g_proj[:, :, 1, 1], g_proj[:, :, 1, 0] - g_proj[:, :, 0, 1]]
    )
    return (
        denoised,
        grad_lift,
        lift_bias.reshape(2, ch),
        grad_mid,
        sums[600].reshape(2, ch),
        grad_proj,
    )


def solution(mesh):
    in_specs = (
        P(None, "date", "row", "col"),
        P("date", None),
        P(None, "date", "row", "col"),
        P(),
        P(),
        P(),
        P(),
        P(),
    )
    out_specs = (P(None, "date", "row", "col"), P(), P(), P(), P(), P())
    return jax.shard_map(local, mesh=mesh, in_specs=in_specs, out_specs=out_specs, check_vma=False)
```

```python
import functools
import math

import jax
import jax.numpy as jnp
from jax import lax
from jax.experimental import pallas as pl
from jax.experimental.pallas import tpu as pltpu
from jax.sharding import PartitionSpec as P

MESH = pl.DeviceIdType.MESH

LR = 2
LC = 4


def mm(a, b):
    return jnp.dot(a, b, preferred_element_type=jnp.float32)


def mm_t(a, b):
    return lax.dot_general(a, b, (((1,), (1,)), ((), ())), preferred_element_type=jnp.float32)


def step_kernel(
    dims, scale,
    slc_ref, pick_ref, avg_ref, tgt_ref, wl_any, bl_any, wmid_any, bmid_any, wproj_any,
    den_ref, o_ref, small_ref,
    pool, look_f, look_s, look_r, tgt_r, fld, tfld, i3a, i3b, h2s, tsum, dn3, dnm3, dp2m, dp1, outs, x_ref,
    wl_in, bl_in, wm_in, bm_in, wj_in, w_sem, w1_ref, wp_ref, wpb_ref, wf_ref, wb_ref, bm_ref, wtmp,
    plane_in, date_in, small_in, small_date, small_sem, small_date_sem, slab_sem, look_sem, tgt_sem, den_sem, plane_sem, date_sem, gather_sem,
):
    n_row, n_col, n_date, pp, tr, tc = dims
    r, c, d = lax.axis_index("row"), lax.axis_index("col"), lax.axis_index("date")
    n_plane = n_row * n_col
    me = r * n_col + c
    rows = n_row * tr
    gap = rows + 1
    nb = gap * pp
    n = nb * 128
    base = (128 - tc) // 2
    pairs = pp * n_row
    f32, bf16 = jnp.float32, jnp.bfloat16

    def plane_peer(k):
        peer = lax.rem(me + k, n_plane)
        return peer, (lax.div(peer, n_col), lax.rem(peer, n_col), d)

    def date_peer(k):
        return (r, c, lax.rem(d + k, n_date))

    def remote(src, dst, sems, at, where):
        copy = pltpu.make_async_remote_copy(
            src_ref=src, dst_ref=dst, send_sem=sems.at[0, at], recv_sem=sems.at[1, at],
            device_id=where, device_id_type=MESH,
        )
        copy.start()
        return copy

    fetches = []
    wide = zip((wl_any, bl_any, wmid_any, bmid_any, wproj_any), (wl_in, bl_in, wm_in, bm_in, wj_in))
    for k, (src, dst) in enumerate(wide):
        copy = pltpu.make_async_copy(src, dst, w_sem.at[k])
        copy.start()
        fetches.append(copy)
    barrier = pltpu.get_barrier_semaphore()
    for k in range(1, n_plane):
        pl.semaphore_signal(barrier, inc=1, device_id=plane_peer(k)[1], device_id_type=MESH)
    for k in range(1, n_date):
        pl.semaphore_signal(barrier, inc=1, device_id=date_peer(k), device_id_type=MESH)
    pl.semaphore_wait(barrier, n_plane + n_date - 2)

    sent = []
    slabs = [remote(slc_ref, pool.at[k - 1], slab_sem, k, date_peer(n_date - k)) for k in (1, 2)]

    def exchange(src, dst, sems):
        copies = []
        for way in range(3):
            col = lax.rem(c + (0, 1, n_col - 1)[way], n_col)
            for o in range(n_row):
                k = lax.rem(r + o, n_row)
                at = way * n_row + o
                if way == 0 and o == 0:
                    copy = pltpu.make_async_copy(src.at[k], dst.at[0, r], sems.at[0, at])
                    copy.start()
                    copies.append((copy, True))
                else:
                    copies.append((remote(src.at[k], dst.at[way, r], sems, at, (k, col, d)), False))
        return copies

    tgt_copies = exchange(tgt_ref, tgt_r, tgt_sem)
    for ref in (fld, tfld, dn3, dnm3, tsum):
        ref[...] = jnp.zeros_like(ref)
    edge = jnp.zeros((i3a.shape[0], 128), bf16)
    for ref in (i3a, i3b):
        ref[:, 0:128] = edge
        ref[:, (nb + 1) * 128 : (nb + 2) * 128] = edge
    x_ref[...] = jnp.zeros_like(x_ref)
    lane = lax.broadcasted_iota(jnp.int32, (1, 128), 1)
    spot = c * tc + lane - base
    inside = (spot >= 0) & (spot < n_col * tc)
    own = (lane >= base) & (lane < base + tc)
    for copy in fetches:
        copy.wait()
    wtmp[...] = jnp.zeros_like(wtmp)

    def joined(a, b):
        return jnp.concatenate([a, b], axis=1)

    for t in range(3):
        for u in range(3):
            pair = wl_in[t, u].astype(f32)
            at = 8 * t + 2 * u
            wtmp[0, at : at + 1, :] = joined(pair[0:1], pair[1:2])
            wtmp[0, at + 1 : at + 2, :] = joined(-pair[1:2], pair[0:1])
            pair = wj_in[t, u].astype(f32)
            real, imag = joined(pair[0:1], -pair[1:2]), joined(pair[1:2], pair[0:1])
            flip = 8 * (2 - t) + 2 * (2 - u)
            wtmp[1, at : at + 1, :] = real
            wtmp[1, at + 1 : at + 2, :] = imag
            wtmp[2, flip : flip + 1, :] = real
            wtmp[2, flip + 1 : flip + 2, :] = imag
            wr, wi = wm_in[0, t, u].astype(f32), wm_in[1, t, u].astype(f32)
            block = jnp.concatenate([joined(wr, wi), joined(-wi, wr)], axis=0)
            wb_ref[2 - t, :, (2 - u) * 128 : (3 - u) * 128] = block.astype(bf16)
            wf_ref[t, :, u * 128 : (u + 1) * 128] = block.T.astype(bf16)
    bias = bl_in[...].astype(f32)
    wtmp[0, 14:15, :] = joined(bias[0:1], bias[1:2])
    bias = bm_in[...].astype(f32)
    wtmp[3, 0:1, :] = joined(bias[0:1], bias[1:2])
    w1_ref[...] = wtmp[0].T[:, 0:32].astype(bf16)
    wp_ref[...] = wtmp[1, 0:32].astype(bf16)
    wpb_ref[...] = wtmp[2].T[:, 0:32].astype(bf16)
    bm_ref[...] = wtmp[3].T[:, 0:1]
    for copy in slabs:
        copy.wait_recv()
    sent += slabs

    depth = slc_ref.shape[0]
    picked = (
        mm(pick_ref[:, :depth], slc_ref[...])
        + mm(pick_ref[:, depth : 2 * depth], pool[0])
        + mm(pick_ref[:, 2 * depth :], pool[1])
    )
    parts = slc_ref.shape[1] // (LR * tr)
    halves = tc * LC // parts
    sides = []
    for h in range(halves):
        at = [picked[q * pairs : (q + 1) * pairs] for q in (h, halves + h, 2 * halves + h, 3 * halves + h)]
        a0, a1, b0, b1 = at
        rowsum = []
        for prod in (a0 * b0 + a1 * b1, a1 * b0 - a0 * b1):
            for t in range(tr):
                rowsum.append(
                    sum(prod[:, (t * LR + q) * parts : (t * LR + q + 1) * parts] for q in range(LR))
                )
        sides.append(jnp.concatenate(rowsum, axis=0))
    looked = jnp.dot(
        jnp.concatenate(sides, axis=1), avg_ref[...],
        precision=lax.Precision.HIGHEST, preferred_element_type=f32,
    )
    look_f[...] = jnp.zeros_like(look_f)
    for k in range(n_row):
        for q in range(2 * tr):
            look_f[k, q * pp : (q + 1) * pp, :] = looked[q * pairs + k * pp : q * pairs + (k + 1) * pp]
    look_s[...] = look_f[...].astype(bf16)
    look_copies = exchange(look_s, look_r, look_sem)

    def settle(copies):
        for copy, near in copies:
            if near:
                copy.wait()
            else:
                copy.wait_recv()
                sent.append(copy)

    def assemble(ref, s):
        mid = pltpu.roll(ref[0, s].astype(f32), base, 1)
        low = pltpu.roll(ref[1, s].astype(f32), (base - tc) % 128, 1)
        high = pltpu.roll(ref[2, s].astype(f32), base + tc, 1)
        joined = jnp.where(own, mid, jnp.where(lane < base, low, high))
        near = (lane >= base - 5) & (lane < base + tc + 5)
        return jnp.where(inside & near, joined, 0.0)

    settle(tgt_copies)
    for s in range(n_row):
        block = assemble(tgt_r, s)
        for z in range(2):
            for t in range(tr):
                for p in range(pp):
                    i = (z * tr + t) * pp + p
                    b = p * gap + s * tr + t
                    tfld[z : z + 1, b * 128 : (b + 1) * 128] = block[i : i + 1]
    settle(look_copies)
    for s in range(n_row):
        block = assemble(look_r, s)
        for u, turned in enumerate((pltpu.roll(block, 1, 1), block, pltpu.roll(block, 127, 1))):
            for z in range(2):
                for t in range(tr):
                    for p in range(pp):
                        i = (z * tr + t) * pp + p
                        b = p * gap + s * tr + t + 1
                        fld[2 * u + z : 2 * u + z + 1, b * 128 : (b + 1) * 128] = turned[i : i + 1]
    fld[6:7, :] = jnp.ones((1, (nb + 2) * 128), f32)

    def taps(ref, at, width):
        three = [ref[:, pl.ds(pl.multiple_of(at + t * 128, 128), width)] for t in range(3)]
        return jnp.concatenate(three + [jnp.zeros((8, width), f32)], axis=0).astype(bf16)

    def turned_store(ref, value, at):
        for u, turn in enumerate((1, 0, 127)):
            for q in range(2):
                piece = value[:, q * 128 : (q + 1) * 128]
                if turn:
                    piece = pltpu.roll(piece, turn, 1)
                ref[u * 128 : (u + 1) * 128, pl.ds(pl.multiple_of(at + (q + 1) * 128, 128), 128)] = (
                    piece.astype(bf16)
                )

    def good(b):
        one = [inside & (lax.rem(b + q, gap) != gap - 1) for q in range(2)]
        return jnp.concatenate(one, axis=1)

    own2 = jnp.concatenate([own, own], axis=1)

    def rounded(value):
        return value.astype(bf16).astype(f32)

    def lift(i, carry):
        at = pl.multiple_of(i * 256, 256)
        pre1 = mm(w1_ref[...], taps(fld, at, 256))
        turned_store(i3a, rounded(jnp.where(good(2 * i), jnp.maximum(pre1, 0.0), 0.0)), at)
        return carry

    lax.fori_loop(0, nb // 2, lift, 0, unroll=True)

    def conv(w_ref, ref, at):
        total = 0.0
        for t in range(3):
            total = total + mm(w_ref[t], ref[:, pl.ds(pl.multiple_of(at + t * 128, 128), 256)])
        return total

    def mid(i, carry):
        at = pl.multiple_of(i * 256, 256)
        pre2 = conv(wf_ref, i3a, at) + bm_ref[...]
        h2 = jnp.where(good(2 * i), jnp.maximum(pre2, 0.0), 0.0).astype(bf16)
        h2s[:, pl.ds(at, 256)] = h2
        tsum[:, pl.ds(pl.multiple_of(at + 128, 128), 256)] = mm(wp_ref[...], h2)
        return carry

    lax.fori_loop(0, nb // 2, mid, 0, unroll=True)

    six = sum(tsum[8 * t : 8 * t + 8, t * 128 : t * 128 + n] for t in range(3))
    noise = pltpu.roll(six, 1, 1)[0:2] + six[2:4] + pltpu.roll(six, n - 1, 1)[4:6]
    den = fld[2:4, 128 : 128 + n] - noise
    shifted = pltpu.roll(den, n - base, 1)
    outs[...] = jnp.zeros_like(outs)
    for s in range(n_row):
        for z in range(2):
            for t in range(tr):
                for p in range(pp):
                    i = (z * tr + t) * pp + p
                    b = p * gap + s * tr + t
                    outs[s, i : i + 1, :] = shifted[z : z + 1, b * 128 : (b + 1) * 128]
    den_copies = []
    for o in range(n_row):
        k = lax.rem(r + o, n_row)
        if o == 0:
            copy = pltpu.make_async_copy(outs.at[k], den_ref.at[r], den_sem.at[0, o])
            copy.start()
            den_copies.append((copy, True))
        else:
            den_copies.append((remote(outs.at[k], den_ref.at[r], den_sem, o, (k, c, d)), False))
    dn = rounded((tfld[0:2, :] - den) * scale)
    rowok = [jnp.full((1, 128), b % gap != gap - 1) for b in range(nb)]
    mask = jnp.concatenate([inside & ok for ok in rowok], axis=1)
    own_all = jnp.concatenate([own & ok for ok in rowok], axis=1)
    for ref, keep in ((dn3, mask), (dnm3, own_all)):
        kept = jnp.where(keep, dn, 0.0)
        ref[0:2, 128 : 128 + n] = pltpu.roll(kept, 1, 1)
        ref[2:4, 128 : 128 + n] = kept
        ref[4:6, 128 : 128 + n] = pltpu.roll(kept, n - 1, 1)

    def back2(i, carry):
        at = pl.multiple_of(i * 256, 256)
        grad = mm(wpb_ref[...], taps(dn3, at, 256))
        grad = rounded(jnp.where(h2s[:, pl.ds(at, 256)].astype(f32) > 0, grad, 0.0))
        turned_store(i3b, grad, at)
        dp2m[:, pl.ds(at, 256)] = jnp.where(own2, grad, 0.0).astype(bf16)
        return carry

    lax.fori_loop(0, nb // 2, back2, 0, unroll=True)

    sign = jnp.where(lane < 64, 1.0, -1.0)
    for t in range(3):
        gram = mm_t(i3a[:, t * 128 : t * 128 + n], dp2m[...])
        for u in range(3):
            upper = gram[u * 128 : u * 128 + 64]
            lower = gram[u * 128 + 64 : u * 128 + 128]
            x_ref[(3 * t + u) * 64 : (3 * t + u) * 64 + 64, :] = upper + sign * pltpu.roll(lower, 64, 1)
    x_ref[576:600, :] = mm_t(taps(dnm3, 0, n), h2s[...])[0:24]
    x_ref[600:608, :] = mm_t(jnp.ones((16, n), bf16), dp2m[...])[0:8]

    piece = plane_in.shape[1]

    def slot(ref, k):
        return ref.at[pl.ds(pl.multiple_of(k * piece, 8), piece)]

    scatter = []
    for k in range(1, n_plane):
        peer, where = plane_peer(k)
        scatter.append(remote(slot(x_ref, peer), plane_in.at[k], plane_sem, k, where))

    def back1(i, carry):
        at = pl.multiple_of(i * 256, 256)
        h1 = i3a[128:256, pl.ds(pl.multiple_of(at + 128, 128), 256)].astype(f32)
        grad = jnp.where((h1 > 0) & own2, conv(wb_ref, i3b, at), 0.0)
        dp1[:, pl.ds(at, 256)] = grad.astype(bf16)
        return carry

    lax.fori_loop(0, nb // 2, back1, 0, unroll=True)

    small_in[me] = mm_t(taps(fld, 0, n), dp1[...])[0:24]
    small = [
        remote(small_in.at[me], small_in.at[me], small_sem, k, plane_peer(k)[1]) for k in range(1, n_plane)
    ]
    part = slot(x_ref, me)[...]
    for k, copy in zip(range(1, n_plane), scatter):
        copy.wait_recv()
        part = part + plane_in[k]
    date_in[d] = part
    spread = [remote(date_in.at[d], date_in.at[d], date_sem, k, date_peer(k)) for k in range(1, n_date)]

    def total(ref, count):
        return functools.reduce(lambda a, b: a + b, [ref[k] for k in range(count)])

    for copy in small:
        copy.wait_recv()
    small_date[d] = total(small_in, n_plane)
    small_spread = [
        remote(small_date.at[d], small_date.at[d], small_date_sem, k, date_peer(k)) for k in range(1, n_date)
    ]
    for copy in spread:
        copy.wait_recv()
    slot(o_ref, me)[...] = total(date_in, n_date)
    gather = [
        remote(slot(o_ref, me), slot(o_ref, me), gather_sem, k, plane_peer(k)[1])
        for k in range(1, n_plane)
    ]
    for copy in small_spread:
        copy.wait_recv()
    small_ref[...] = total(small_date, n_date)
    settle(den_copies)
    for copy in gather:
        copy.wait_recv()
    for copy in sent + scatter + small + spread + small_spread + gather:
        copy.wait_send()


def local(slc, pairs, target, w_lift, b_lift, w_mid, b_mid, w_proj):
    n_row, n_col, n_date = (lax.axis_size(axis) for axis in ("row", "col", "date"))
    dates, srows, scols = slc.shape[1:]
    count, tr, tc = target.shape[1:]
    ch = w_mid.shape[-1]
    pp = count // n_row
    halves = scols // 128
    bf16, f32 = jnp.bfloat16, jnp.float32
    rows = 2 * tr * pp
    pad_rows = -(-rows // 16) * 16
    packed = slc.reshape(2, dates, srows, halves, 128).transpose(1, 0, 3, 2, 4)
    packed = packed.reshape(dates * 2 * halves, srows * 128)
    index = (pairs - lax.axis_index("date") * dates).T
    kinds = 2 * halves
    want = (index[:, None, :] * kinds + jnp.arange(kinds, dtype=jnp.int32)[None, :, None]).reshape(-1)
    pick = (want[:, None] == jnp.arange(3 * dates * kinds, dtype=jnp.int32)[None, :]).astype(bf16)
    spots = jnp.arange(scols, dtype=jnp.int32)[:, None] // LC
    avg = jnp.where(spots == jnp.arange(128, dtype=jnp.int32)[None, :], 1.0 / (LR * LC), 0.0).astype(f32)
    tgt = target.reshape(2, n_row, pp, tr, tc).transpose(1, 0, 3, 2, 4).reshape(n_row, rows, tc)
    tgt = jnp.pad(tgt, ((0, 0), (0, pad_rows - rows), (0, 128 - tc)))
    w_lift, w_proj = w_lift.transpose(1, 2, 0, 3), w_proj.transpose(1, 2, 0, 3)
    scale = 1.0 / math.sqrt(2.0 * count * n_date * tr * n_row * tc * n_col)
    nb = (n_row * tr + 1) * pp
    n, wide = nb * 128, (nb + 2) * 128
    n_plane = n_row * n_col
    piece = -(-608 // (8 * n_plane)) * 8
    dma = pltpu.SemaphoreType.DMA
    vmem = pltpu.VMEM
    den, sums, small = pl.pallas_call(
        functools.partial(step_kernel, (n_row, n_col, n_date, pp, tr, tc), scale),
        out_shape=(
            jax.ShapeDtypeStruct((n_row, pad_rows, 128), f32),
            jax.ShapeDtypeStruct((n_plane * piece, 128), f32),
            jax.ShapeDtypeStruct((24, 128), f32),
        ),
        in_specs=[pl.BlockSpec(memory_space=vmem)] * 4 + [pl.BlockSpec(memory_space=pl.ANY)] * 5,
        out_specs=(pl.BlockSpec(memory_space=vmem),) * 3,
        scratch_shapes=[
            vmem((2,) + packed.shape, bf16),
            vmem((n_row, pad_rows, 128), f32),
            vmem((n_row, pad_rows, 128), bf16),
            vmem((3, n_row, pad_rows, 128), bf16),
            vmem((3, n_row, pad_rows, 128), f32),
            vmem((8, wide), f32),
            vmem((8, n), f32),
            vmem((6 * ch, wide), bf16),
            vmem((6 * ch, wide), bf16),
            vmem((2 * ch, n), bf16),
            vmem((32, wide), f32),
            vmem((8, wide), f32),
            vmem((8, wide), f32),
            vmem((2 * ch, n), bf16),
            vmem((2 * ch, n), bf16),
            vmem((n_row, pad_rows, 128), f32),
            vmem((n_plane * piece, 128), f32),
            vmem(w_lift.shape, bf16),
            vmem(b_lift.shape, bf16),
            vmem(w_mid.shape, bf16),
            vmem(b_mid.shape, bf16),
            vmem(w_proj.shape, bf16),
            dma((5,)),
            vmem((2 * ch, 32), bf16),
            vmem((32, 2 * ch), bf16),
            vmem((2 * ch, 32), bf16),
            vmem((3, 2 * ch, 6 * ch), bf16),
            vmem((3, 2 * ch, 6 * ch), bf16),
            vmem((2 * ch, 1), f32),
            vmem((4, 128, 128), f32),
            vmem((n_plane, piece, 128), f32),
            vmem((n_date, piece, 128), f32),
            vmem((n_plane, 24, 128), f32),
            vmem((n_date, 24, 128), f32),
            dma((2, n_plane)),
            dma((2, n_date)),
            dma((2, 3)),
            dma((2, 3 * n_row)),
            dma((2, 3 * n_row)),
            dma((2, n_row)),
            dma((2, n_plane)),
            dma((2, n_date)),
            dma((2, n_plane)),
        ],
        compiler_params=pltpu.CompilerParams(
            collective_id=0, has_side_effects=True, vmem_limit_bytes=48 * 1024 * 1024
        ),
    )(packed, pick, avg, tgt, w_lift, b_lift, w_mid, b_mid, w_proj)
    denoised = den[:, :rows, :tc].reshape(n_row, 2, tr, pp, tc).transpose(1, 0, 3, 2, 4)
    denoised = denoised.reshape(2, count, tr, tc)
    grad_mid = sums[: 9 * ch].reshape(3, 3, ch, 2, ch).transpose(3, 0, 1, 2, 4)
    g_lift = small.reshape(3, 8, 2 * ch)
    lift_bias = g_lift[1, 6]
    g_lift = g_lift[:, :6].reshape(3, 3, 2, 2, ch)
    grad_lift = jnp.stack(
        [g_lift[:, :, 0, 0] + g_lift[:, :, 1, 1], g_lift[:, :, 0, 1] - g_lift[:, :, 1, 0]]
    )
    g_proj = sums[576:600].reshape(3, 8, 2 * ch)[:, :6].reshape(3, 3, 2, 2, ch)[::-1, ::-1]
    grad_proj = jnp.stack(
        [g_proj[:, :, 0, 0] + g_proj[:, :, 1, 1], g_proj[:, :, 1, 0] - g_proj[:, :, 0, 1]]
    )
    return (
        denoised,
        grad_lift,
        lift_bias.reshape(2, ch),
        grad_mid,
        sums[600].reshape(2, ch),
        grad_proj,
    )


def solution(mesh):
    in_specs = (
        P(None, "date", "row", "col"),
        P("date", None),
        P(None, "date", "row", "col"),
        P(),
        P(),
        P(),
        P(),
        P(),
    )
    out_specs = (P(None, "date", "row", "col"), P(), P(), P(), P(), P())
    return jax.shard_map(local, mesh=mesh, in_specs=in_specs, out_specs=out_specs, check_vma=False)
```

```python
import functools
import math

import jax
import jax.numpy as jnp
from jax import lax
from jax.experimental import pallas as pl
from jax.experimental.pallas import tpu as pltpu
from jax.sharding import PartitionSpec as P

MESH = pl.DeviceIdType.MESH

LR = 2
LC = 4


def mm(a, b):
    return jnp.dot(a, b, preferred_element_type=jnp.float32)


def mm_t(a, b):
    return lax.dot_general(a, b, (((1,), (1,)), ((), ())), preferred_element_type=jnp.float32)


def step_kernel(
    dims, scale,
    slc_ref, pick_ref, avg_ref, tgt_ref, wl_any, bl_any, wmid_any, bmid_any, wproj_any,
    den_ref, o_ref, small_ref,
    pool, look_f, look_s, look_r, tgt_r, fld, tfld, i3a, i3b, h2s, tsum, dn3, dnm3, dp2m, dp1, outs, x_ref,
    wl_in, bl_in, wm_in, bm_in, wj_in, w_sem, w1_ref, wp_ref, wpb_ref, wf_ref, wb_ref, bm_ref, wtmp,
    plane_in, date_in, small_in, small_date, small_sem, small_date_sem, slab_sem, look_sem, tgt_sem, den_sem, plane_sem, date_sem, gather_sem,
):
    n_row, n_col, n_date, pp, tr, tc = dims
    r, c, d = lax.axis_index("row"), lax.axis_index("col"), lax.axis_index("date")
    n_plane = n_row * n_col
    me = r * n_col + c
    rows = n_row * tr
    gap = rows + 1
    nb = gap * pp
    n = nb * 128
    base = (128 - tc) // 2
    pairs = pp * n_row
    f32, bf16 = jnp.float32, jnp.bfloat16

    def plane_peer(k):
        peer = lax.rem(me + k, n_plane)
        return peer, (lax.div(peer, n_col), lax.rem(peer, n_col), d)

    def date_peer(k):
        return (r, c, lax.rem(d + k, n_date))

    def remote(src, dst, sems, at, where):
        copy = pltpu.make_async_remote_copy(
            src_ref=src, dst_ref=dst, send_sem=sems.at[0, at], recv_sem=sems.at[1, at],
            device_id=where, device_id_type=MESH,
        )
        copy.start()
        return copy

    fetches = []
    wide = zip((wl_any, bl_any, wmid_any, bmid_any, wproj_any), (wl_in, bl_in, wm_in, bm_in, wj_in))
    for k, (src, dst) in enumerate(wide):
        copy = pltpu.make_async_copy(src, dst, w_sem.at[k])
        copy.start()
        fetches.append(copy)
    barrier = pltpu.get_barrier_semaphore()
    for k in range(1, n_plane):
        pl.semaphore_signal(barrier, inc=1, device_id=plane_peer(k)[1], device_id_type=MESH)
    for k in range(1, n_date):
        pl.semaphore_signal(barrier, inc=1, device_id=date_peer(k), device_id_type=MESH)
    pl.semaphore_wait(barrier, n_plane + n_date - 2)

    sent = []
    slabs = [remote(slc_ref, pool.at[k - 1], slab_sem, k, date_peer(n_date - k)) for k in (1, 2)]

    def exchange(src, dst, sems):
        copies = []
        for way in range(3):
            col = lax.rem(c + (0, 1, n_col - 1)[way], n_col)
            for o in range(n_row):
                k = lax.rem(r + o, n_row)
                at = way * n_row + o
                if way == 0 and o == 0:
                    copy = pltpu.make_async_copy(src.at[k], dst.at[0, r], sems.at[0, at])
                    copy.start()
                    copies.append((copy, True))
                else:
                    copies.append((remote(src.at[k], dst.at[way, r], sems, at, (k, col, d)), False))
        return copies

    tgt_copies = exchange(tgt_ref, tgt_r, tgt_sem)
    for ref in (fld, tfld, dn3, dnm3, tsum):
        ref[...] = jnp.zeros_like(ref)
    edge = jnp.zeros((i3a.shape[0], 128), bf16)
    for ref in (i3a, i3b):
        ref[:, 0:128] = edge
        ref[:, (nb + 1) * 128 : (nb + 2) * 128] = edge
    x_ref[...] = jnp.zeros_like(x_ref)
    lane = lax.broadcasted_iota(jnp.int32, (1, 128), 1)
    spot = c * tc + lane - base
    inside = (spot >= 0) & (spot < n_col * tc)
    own = (lane >= base) & (lane < base + tc)
    for copy in fetches:
        copy.wait()
    wtmp[...] = jnp.zeros_like(wtmp)

    def joined(a, b):
        return jnp.concatenate([a, b], axis=1)

    for t in range(3):
        for u in range(3):
            pair = wl_in[t, u].astype(f32)
            at = 8 * t + 2 * u
            wtmp[0, at : at + 1, :] = joined(pair[0:1], pair[1:2])
            wtmp[0, at + 1 : at + 2, :] = joined(-pair[1:2], pair[0:1])
            pair = wj_in[t, u].astype(f32)
            real, imag = joined(pair[0:1], -pair[1:2]), joined(pair[1:2], pair[0:1])
            flip = 8 * (2 - t) + 2 * (2 - u)
            wtmp[1, at : at + 1, :] = real
            wtmp[1, at + 1 : at + 2, :] = imag
            wtmp[2, flip : flip + 1, :] = real
            wtmp[2, flip + 1 : flip + 2, :] = imag
            wr, wi = wm_in[0, t, u].astype(f32), wm_in[1, t, u].astype(f32)
            block = jnp.concatenate([joined(wr, wi), joined(-wi, wr)], axis=0)
            wb_ref[2 - t, :, (2 - u) * 128 : (3 - u) * 128] = block.astype(bf16)
            wf_ref[t, :, u * 128 : (u + 1) * 128] = block.T.astype(bf16)
    bias = bl_in[...].astype(f32)
    wtmp[0, 14:15, :] = joined(bias[0:1], bias[1:2])
    bias = bm_in[...].astype(f32)
    wtmp[3, 0:1, :] = joined(bias[0:1], bias[1:2])
    w1_ref[...] = wtmp[0].T[:, 0:32].astype(bf16)
    wp_ref[...] = wtmp[1, 0:32].astype(bf16)
    wpb_ref[...] = wtmp[2].T[:, 0:32].astype(bf16)
    bm_ref[...] = wtmp[3].T[:, 0:1]
    for copy in slabs:
        copy.wait_recv()
    sent += slabs

    depth = slc_ref.shape[0]
    picked = (
        mm(pick_ref[:, :depth], slc_ref[...])
        + mm(pick_ref[:, depth : 2 * depth], pool[0])
        + mm(pick_ref[:, 2 * depth :], pool[1])
    )
    parts = slc_ref.shape[1] // (LR * tr)
    halves = tc * LC // parts
    sides = []
    for h in range(halves):
        at = [picked[q * pairs : (q + 1) * pairs] for q in (h, halves + h, 2 * halves + h, 3 * halves + h)]
        a0, a1, b0, b1 = at
        rowsum = []
        for prod in (a0 * b0 + a1 * b1, a1 * b0 - a0 * b1):
            for t in range(tr):
                rowsum.append(
                    sum(prod[:, (t * LR + q) * parts : (t * LR + q + 1) * parts] for q in range(LR))
                )
        sides.append(jnp.concatenate(rowsum, axis=0))
    looked = jnp.dot(
        jnp.concatenate(sides, axis=1), avg_ref[...],
        precision=lax.Precision.HIGHEST, preferred_element_type=f32,
    )
    look_f[...] = jnp.zeros_like(look_f)
    for k in range(n_row):
        for q in range(2 * tr):
            look_f[k, q * pp : (q + 1) * pp, :] = looked[q * pairs + k * pp : q * pairs + (k + 1) * pp]
    look_s[...] = look_f[...].astype(bf16)
    look_copies = exchange(look_s, look_r, look_sem)

    def settle(copies):
        for copy, near in copies:
            if near:
                copy.wait()
            else:
                copy.wait_recv()
                sent.append(copy)

    def assemble(ref, s):
        mid = pltpu.roll(ref[0, s].astype(f32), base, 1)
        low = pltpu.roll(ref[1, s].astype(f32), (base - tc) % 128, 1)
        high = pltpu.roll(ref[2, s].astype(f32), base + tc, 1)
        joined = jnp.where(own, mid, jnp.where(lane < base, low, high))
        near = (lane >= base - 5) & (lane < base + tc + 5)
        return jnp.where(inside & near, joined, 0.0)

    settle(tgt_copies)
    for s in range(n_row):
        block = assemble(tgt_r, s)
        for z in range(2):
            for t in range(tr):
                for p in range(pp):
                    i = (z * tr + t) * pp + p
                    b = p * gap + s * tr + t
                    tfld[z : z + 1, b * 128 : (b + 1) * 128] = block[i : i + 1]
    settle(look_copies)
    for s in range(n_row):
        block = assemble(look_r, s)
        for u, turned in enumerate((pltpu.roll(block, 1, 1), block, pltpu.roll(block, 127, 1))):
            for z in range(2):
                for t in range(tr):
                    for p in range(pp):
                        i = (z * tr + t) * pp + p
                        b = p * gap + s * tr + t + 1
                        fld[2 * u + z : 2 * u + z + 1, b * 128 : (b + 1) * 128] = turned[i : i + 1]
    fld[6:7, :] = jnp.ones((1, (nb + 2) * 128), f32)

    def taps(ref, at, width):
        three = [ref[:, pl.ds(pl.multiple_of(at + t * 128, 128), width)] for t in range(3)]
        return jnp.concatenate(three + [jnp.zeros((8, width), f32)], axis=0).astype(bf16)

    def turned_store(ref, value, at):
        for u, turn in enumerate((1, 0, 127)):
            for q in range(2):
                piece = value[:, q * 128 : (q + 1) * 128]
                if turn:
                    piece = pltpu.roll(piece, turn, 1)
                ref[u * 128 : (u + 1) * 128, pl.ds(pl.multiple_of(at + (q + 1) * 128, 128), 128)] = (
                    piece.astype(bf16)
                )

    def good(b):
        one = [inside & (lax.rem(b + q, gap) != gap - 1) for q in range(2)]
        return jnp.concatenate(one, axis=1)

    own2 = jnp.concatenate([own, own], axis=1)

    def rounded(value):
        return value.astype(bf16).astype(f32)

    def lift(i, carry):
        at = pl.multiple_of(i * 256, 256)
        pre1 = mm(w1_ref[...], taps(fld, at, 256))
        turned_store(i3a, rounded(jnp.where(good(2 * i), jnp.maximum(pre1, 0.0), 0.0)), at)
        return carry

    lax.fori_loop(0, nb // 2, lift, 0, unroll=True)

    def conv(w_ref, ref, at):
        total = 0.0
        for t in range(3):
            total = total + mm(w_ref[t], ref[:, pl.ds(pl.multiple_of(at + t * 128, 128), 256)])
        return total

    def mid(i, carry):
        at = pl.multiple_of(i * 256, 256)
        pre2 = conv(wf_ref, i3a, at) + bm_ref[...]
        h2 = jnp.where(good(2 * i), jnp.maximum(pre2, 0.0), 0.0).astype(bf16)
        h2s[:, pl.ds(at, 256)] = h2
        tsum[:, pl.ds(pl.multiple_of(at + 128, 128), 256)] = mm(wp_ref[...], h2)
        return carry

    lax.fori_loop(0, nb // 2, mid, 0, unroll=True)

    six = sum(tsum[8 * t : 8 * t + 8, t * 128 : t * 128 + n] for t in range(3))
    noise = pltpu.roll(six, 1, 1)[0:2] + six[2:4] + pltpu.roll(six, n - 1, 1)[4:6]
    den = fld[2:4, 128 : 128 + n] - noise
    shifted = pltpu.roll(den, n - base, 1)
    outs[...] = jnp.zeros_like(outs)
    for s in range(n_row):
        for z in range(2):
            for t in range(tr):
                for p in range(pp):
                    i = (z * tr + t) * pp + p
                    b = p * gap + s * tr + t
                    outs[s, i : i + 1, :] = shifted[z : z + 1, b * 128 : (b + 1) * 128]
    den_copies = []
    for o in range(n_row):
        k = lax.rem(r + o, n_row)
        if o == 0:
            copy = pltpu.make_async_copy(outs.at[k], den_ref.at[r], den_sem.at[0, o])
            copy.start()
            den_copies.append((copy, True))
        else:
            den_copies.append((remote(outs.at[k], den_ref.at[r], den_sem, o, (k, c, d)), False))
    dn = rounded((tfld[0:2, :] - den) * scale)
    rowok = [jnp.full((1, 128), b % gap != gap - 1) for b in range(nb)]
    mask = jnp.concatenate([inside & ok for ok in rowok], axis=1)
    own_all = jnp.concatenate([own & ok for ok in rowok], axis=1)
    for ref, keep in ((dn3, mask), (dnm3, own_all)):
        kept = jnp.where(keep, dn, 0.0)
        ref[0:2, 128 : 128 + n] = pltpu.roll(kept, 1, 1)
        ref[2:4, 128 : 128 + n] = kept
        ref[4:6, 128 : 128 + n] = pltpu.roll(kept, n - 1, 1)

    def back2(i, carry):
        at = pl.multiple_of(i * 256, 256)
        grad = mm(wpb_ref[...], taps(dn3, at, 256))
        grad = rounded(jnp.where(h2s[:, pl.ds(at, 256)].astype(f32) > 0, grad, 0.0))
        turned_store(i3b, grad, at)
        dp2m[:, pl.ds(at, 256)] = jnp.where(own2, grad, 0.0).astype(bf16)
        return carry

    lax.fori_loop(0, nb // 2, back2, 0, unroll=True)

    sign = jnp.where(lane < 64, 1.0, -1.0)
    for t in range(3):
        gram = mm_t(i3a[:, t * 128 : t * 128 + n], dp2m[...])
        for u in range(3):
            upper = gram[u * 128 : u * 128 + 64]
            lower = gram[u * 128 + 64 : u * 128 + 128]
            x_ref[(3 * t + u) * 64 : (3 * t + u) * 64 + 64, :] = upper + sign * pltpu.roll(lower, 64, 1)
    x_ref[576:600, :] = mm_t(taps(dnm3, 0, n), h2s[...])[0:24]
    x_ref[600:608, :] = mm_t(jnp.ones((16, n), bf16), dp2m[...])[0:8]

    piece = plane_in.shape[1]

    def slot(ref, k):
        return ref.at[pl.ds(pl.multiple_of(k * piece, 8), piece)]

    scatter = []
    for k in range(1, n_plane):
        peer, where = plane_peer(k)
        scatter.append(remote(slot(x_ref, peer), plane_in.at[k], plane_sem, k, where))

    def back1(i, carry):
        at = pl.multiple_of(i * 256, 256)
        h1 = i3a[128:256, pl.ds(pl.multiple_of(at + 128, 128), 256)].astype(f32)
        grad = jnp.where((h1 > 0) & own2, conv(wb_ref, i3b, at), 0.0)
        dp1[:, pl.ds(at, 256)] = grad.astype(bf16)
        return carry

    lax.fori_loop(0, nb // 2, back1, 0, unroll=True)

    small_in[me] = mm_t(taps(fld, 0, n), dp1[...])[0:24]
    small = [
        remote(small_in.at[me], small_in.at[me], small_sem, k, plane_peer(k)[1]) for k in range(1, n_plane)
    ]
    part = slot(x_ref, me)[...]
    for k, copy in zip(range(1, n_plane), scatter):
        copy.wait_recv()
        part = part + plane_in[k]
    date_in[d] = part
    spread = [remote(date_in.at[d], date_in.at[d], date_sem, k, date_peer(k)) for k in range(1, n_date)]

    def total(ref, count):
        return functools.reduce(lambda a, b: a + b, [ref[k] for k in range(count)])

    for copy in small:
        copy.wait_recv()
    small_date[d] = total(small_in, n_plane)
    small_spread = [
        remote(small_date.at[d], small_date.at[d], small_date_sem, k, date_peer(k)) for k in range(1, n_date)
    ]
    for copy in spread:
        copy.wait_recv()
    slot(o_ref, me)[...] = total(date_in, n_date)
    gather = [
        remote(slot(o_ref, me), slot(o_ref, me), gather_sem, k, plane_peer(k)[1])
        for k in range(1, n_plane)
    ]
    for copy in small_spread:
        copy.wait_recv()
    small_ref[...] = total(small_date, n_date)
    settle(den_copies)
    for copy in gather:
        copy.wait_recv()
    for copy in sent + scatter + small + spread + small_spread + gather:
        copy.wait_send()


def finish_kernel(dims, den, sums, small, den_out, lift_out, lbias_out, mid_out, mbias_out, proj_out):
    n_row, pp, tr, tc, ch = dims
    for k in range(n_row):
        for z in range(2):
            for t in range(tr):
                at = (z * tr + t) * pp
                den_out[z, t, k * pp : (k + 1) * pp, :] = den[k, at : at + pp, 0:tc]
    for t in range(3):
        for u in range(3):
            at = 8 * t + 2 * u
            upper, lower = small[at : at + 1, :], small[at + 1 : at + 2, :]
            lift_out[t, u, 0:1, :] = upper[:, 0:ch] + lower[:, ch:]
            lift_out[t, u, 1:2, :] = upper[:, ch:] - lower[:, 0:ch]
            at = 576 + 8 * (2 - t) + 2 * (2 - u)
            upper, lower = sums[at : at + 1, :], sums[at + 1 : at + 2, :]
            proj_out[t, u, 0:1, :] = upper[:, 0:ch] + lower[:, ch:]
            proj_out[t, u, 1:2, :] = lower[:, 0:ch] - upper[:, ch:]
            at = (3 * t + u) * ch
            for z in range(2):
                mid_out[z, t, u] = sums[at : at + ch, z * ch : (z + 1) * ch]
    for z in range(2):
        lbias_out[z : z + 1, :] = small[14:15, z * ch : (z + 1) * ch]
        mbias_out[z : z + 1, :] = sums[600:601, z * ch : (z + 1) * ch]


def local(slc, pairs, target, w_lift, b_lift, w_mid, b_mid, w_proj):
    n_row, n_col, n_date = (lax.axis_size(axis) for axis in ("row", "col", "date"))
    dates, srows, scols = slc.shape[1:]
    count, tr, tc = target.shape[1:]
    ch = w_mid.shape[-1]
    pp = count // n_row
    halves = scols // 128
    bf16, f32 = jnp.bfloat16, jnp.float32
    rows = 2 * tr * pp
    pad_rows = -(-rows // 16) * 16
    packed = slc.reshape(2, dates, srows, halves, 128).transpose(1, 0, 3, 2, 4)
    packed = packed.reshape(dates * 2 * halves, srows * 128)
    index = (pairs - lax.axis_index("date") * dates).T
    kinds = 2 * halves
    want = (index[:, None, :] * kinds + jnp.arange(kinds, dtype=jnp.int32)[None, :, None]).reshape(-1)
    pick = (want[:, None] == jnp.arange(3 * dates * kinds, dtype=jnp.int32)[None, :]).astype(bf16)
    spots = jnp.arange(scols, dtype=jnp.int32)[:, None] // LC
    avg = jnp.where(spots == jnp.arange(128, dtype=jnp.int32)[None, :], 1.0 / (LR * LC), 0.0).astype(f32)
    tgt = target.reshape(2, n_row, pp, tr, tc).transpose(1, 0, 3, 2, 4).reshape(n_row, rows, tc)
    tgt = jnp.pad(tgt, ((0, 0), (0, pad_rows - rows), (0, 128 - tc)))
    w_lift, w_proj = w_lift.transpose(1, 2, 0, 3), w_proj.transpose(1, 2, 0, 3)
    scale = 1.0 / math.sqrt(2.0 * count * n_date * tr * n_row * tc * n_col)
    nb = (n_row * tr + 1) * pp
    n, wide = nb * 128, (nb + 2) * 128
    n_plane = n_row * n_col
    piece = -(-608 // (8 * n_plane)) * 8
    dma = pltpu.SemaphoreType.DMA
    vmem = pltpu.VMEM
    den, sums, small = pl.pallas_call(
        functools.partial(step_kernel, (n_row, n_col, n_date, pp, tr, tc), scale),
        out_shape=(
            jax.ShapeDtypeStruct((n_row, pad_rows, 128), f32),
            jax.ShapeDtypeStruct((n_plane * piece, 128), f32),
            jax.ShapeDtypeStruct((24, 128), f32),
        ),
        in_specs=[pl.BlockSpec(memory_space=vmem)] * 4 + [pl.BlockSpec(memory_space=pl.ANY)] * 5,
        out_specs=(pl.BlockSpec(memory_space=vmem),) * 3,
        scratch_shapes=[
            vmem((2,) + packed.shape, bf16),
            vmem((n_row, pad_rows, 128), f32),
            vmem((n_row, pad_rows, 128), bf16),
            vmem((3, n_row, pad_rows, 128), bf16),
            vmem((3, n_row, pad_rows, 128), f32),
            vmem((8, wide), f32),
            vmem((8, n), f32),
            vmem((6 * ch, wide), bf16),
            vmem((6 * ch, wide), bf16),
            vmem((2 * ch, n), bf16),
            vmem((32, wide), f32),
            vmem((8, wide), f32),
            vmem((8, wide), f32),
            vmem((2 * ch, n), bf16),
            vmem((2 * ch, n), bf16),
            vmem((n_row, pad_rows, 128), f32),
            vmem((n_plane * piece, 128), f32),
            vmem(w_lift.shape, bf16),
            vmem(b_lift.shape, bf16),
            vmem(w_mid.shape, bf16),
            vmem(b_mid.shape, bf16),
            vmem(w_proj.shape, bf16),
            dma((5,)),
            vmem((2 * ch, 32), bf16),
            vmem((32, 2 * ch), bf16),
            vmem((2 * ch, 32), bf16),
            vmem((3, 2 * ch, 6 * ch), bf16),
            vmem((3, 2 * ch, 6 * ch), bf16),
            vmem((2 * ch, 1), f32),
            vmem((4, 128, 128), f32),
            vmem((n_plane, piece, 128), f32),
            vmem((n_date, piece, 128), f32),
            vmem((n_plane, 24, 128), f32),
            vmem((n_date, 24, 128), f32),
            dma((2, n_plane)),
            dma((2, n_date)),
            dma((2, 3)),
            dma((2, 3 * n_row)),
            dma((2, 3 * n_row)),
            dma((2, n_row)),
            dma((2, n_plane)),
            dma((2, n_date)),
            dma((2, n_plane)),
        ],
        compiler_params=pltpu.CompilerParams(
            collective_id=0, has_side_effects=True, vmem_limit_bytes=48 * 1024 * 1024
        ),
    )(packed, pick, avg, tgt, w_lift, b_lift, w_mid, b_mid, w_proj)
    shape = jax.ShapeDtypeStruct
    denoised, grad_lift, lift_bias, grad_mid, mid_bias, grad_proj = pl.pallas_call(
        functools.partial(finish_kernel, (n_row, pp, tr, tc, ch)),
        out_shape=(
            shape((2, tr, count, tc), f32),
            shape((3, 3, 2, ch), f32),
            shape((2, ch), f32),
            shape((2, 3, 3, ch, ch), f32),
            shape((2, ch), f32),
            shape((3, 3, 2, ch), f32),
        ),
        in_specs=[pl.BlockSpec(memory_space=vmem)] * 3,
        out_specs=(pl.BlockSpec(memory_space=vmem),) * 6,
        compiler_params=pltpu.CompilerParams(vmem_limit_bytes=8 * 1024 * 1024),
    )(den, sums, small)
    return (
        denoised.transpose(0, 2, 1, 3),
        grad_lift.transpose(2, 0, 1, 3),
        lift_bias,
        grad_mid,
        mid_bias,
        grad_proj.transpose(2, 0, 1, 3),
    )


def solution(mesh):
    in_specs = (
        P(None, "date", "row", "col"),
        P("date", None),
        P(None, "date", "row", "col"),
        P(),
        P(),
        P(),
        P(),
        P(),
    )
    out_specs = (P(None, "date", "row", "col"), P(), P(), P(), P(), P())
    return jax.shard_map(local, mesh=mesh, in_specs=in_specs, out_specs=out_specs, check_vma=False)
```
